128 devices in a mesh: bx: 16 (over y, x), by: 8 (over z, core).
Axes of the slice: x: 4, y: 4, z: 4, core: 2. Of those that a mesh axis runs over, the one named last changes fastest.
Arguments:
- right_sides: float32 [16, 8, 128, 768], P('bx', 'by'), may hold values from -6 to 6
- skeleton_order: int32 [16, 8, 4, 768], P('bx', 'by'), may hold values from 0 to 767, as said below
- interp_first: float32 [16, 8, 384, 384], P('bx', 'by'), may hold values from -0.15625 to 0.15625
- interp_second: float32 [16, 8, 384, 192], P('bx', 'by'), may hold values from -0.15625 to 0.15625
- interp_third: float32 [16, 8, 384, 96], P('bx', 'by'), may hold values from -0.15625 to 0.15625
- interp_fourth: float32 [16, 8, 384, 48], P('bx', 'by'), may hold values from -0.15625 to 0.15625
- inverse_first: float32 [16, 8, 384, 384], P('bx', 'by'), may hold values from -0.25 to 0.25
- inverse_second: float32 [16, 8, 384, 192], P('bx', 'by'), may hold values from -0.25 to 0.25
- inverse_third: float32 [16, 8, 384, 96], P('bx', 'by'), may hold values from -0.25 to 0.25
- inverse_fourth: float32 [16, 8, 384, 48], P('bx', 'by'), may hold values from -0.25 to 0.25
- couple_first: float32 [16, 8, 5, 384, 384], P('bx', 'by'), may hold values from -0.09375 to 0.09375
- couple_second: float32 [16, 8, 5, 384, 192], P('bx', 'by'), may hold values from -0.09375 to 0.09375
- couple_third: float32 [16, 8, 5, 384, 96], P('bx', 'by'), may hold values from -0.09375 to 0.09375
- couple_fourth: float32 [16, 8, 5, 384, 48], P('bx', 'by'), may hold values from -0.09375 to 0.09375
- root_inverse: float32 [16, 8, 384, 48], P('bx', 'by'), may hold values from -0.21875 to 0.21875
Outputs:
- solution: float32 [16, 8, 128, 768], P('bx', 'by')
The draws below stay inside these ranges and needn't reach their ends.
Inputs may be any that keep to these rules, and one draw needn't show every extreme that they name: For every fine box and level l, skeleton_order[i, j, l, :] is a permutation of 0 to 767, the same at all fine boxes of one level-l box.
All inputs are finite; a program needn't handle non-finite values.
Results may differ from the reference program's by a relative error of at most 0.0003.
Values sent between devices are 32-bit elements; how exact they have to be, the bound alone decides.
No kernel may reach another device: no remote copies, remote signals or barrier semaphores. Data moves between devices by JAX's collectives and lax.ppermute only.
A program may use at most 128 MiB of HBM per device.

```python
import jax
import jax.numpy as jnp
from jax import lax

SKEL = 384
BOX = 768
NRHS = 128
BOXES_X = 16
BOXES_Y = 8


def draw_skeleton_order(key, part):
    stacked = []
    for level_index, extent in enumerate(((1, 1), (1, 2), (2, 2), (2, 4))):
        group_x, group_y = extent
        box_count = BOXES_X // group_x * (BOXES_Y // group_y)
        subkeys = jax.random.split(jax.random.fold_in(key, level_index + 11), box_count)
        shuffles = jax.vmap(lambda subkey: jax.random.permutation(subkey, BOX))(subkeys)
        layout = shuffles.reshape(BOXES_X // group_x, BOXES_Y // group_y, BOX)
        layout = jnp.repeat(jnp.repeat(layout, group_x, axis=0), group_y, axis=1)
        stacked.append(layout)
    return jnp.stack(stacked, axis=2).astype(jnp.int32)


def level_of(rng, shape, shards, low, high):
    def one(axis_at, shards_of):
        steps = jax.random.uniform(jax.random.fold_in(jax.random.fold_in(rng, 6), axis_at), (shards_of,), jnp.float32, low / len(shards), high / len(shards))
        return jnp.repeat(jnp.exp(steps), shape[axis_at] // shards_of).reshape((-1,) + (1,) * (len(shape) - axis_at - 1))

    loudness = one(*shards[0])
    for cut in shards[1:]:
        loudness = loudness * one(*cut)
    return loudness


def scatter_about(stream_key, shape, deviation, bound, cuts=(), held_as=jnp.bfloat16):
    values = deviation * jax.random.normal(stream_key, shape, jnp.float32)
    if cuts:
        values = values * level_of(stream_key, shape, cuts, -0.22, 0.18)
    return jnp.clip(values, -bound, bound).astype(held_as)


def setup_inputs(seed: int = 0) -> dict:
    keys = jax.random.split(jax.random.key(seed), 16)
    return {
        "right_sides": scatter_about(keys[0], (BOXES_X, BOXES_Y, NRHS, BOX), 1.0, 6.0, ((0, 16), (1, 8)), jnp.float32),
        "skeleton_order": draw_skeleton_order(jax.random.fold_in(keys[15], 71), 0),
        "interp_first": scatter_about(keys[2], (BOXES_X, BOXES_Y, SKEL, SKEL), (4 * SKEL) ** -0.5, 0.15625, ((0, 16), (1, 8)), jnp.float32),
        "interp_second": scatter_about(keys[3], (BOXES_X, BOXES_Y, SKEL, SKEL // 2), (4 * SKEL) ** -0.5, 0.15625, ((0, 16), (1, 8)), jnp.float32),
        "interp_third": scatter_about(keys[4], (BOXES_X, BOXES_Y, SKEL, SKEL // 4), (4 * SKEL) ** -0.5, 0.15625, ((0, 16), (1, 8)), jnp.float32),
        "interp_fourth": scatter_about(keys[5], (BOXES_X, BOXES_Y, SKEL, SKEL // 8), (4 * SKEL) ** -0.5, 0.15625, ((0, 16), (1, 8)), jnp.float32),
        "inverse_first": scatter_about(keys[6], (BOXES_X, BOXES_Y, SKEL, SKEL), (SKEL * 5 // 4) ** -0.5, 0.25, ((0, 16), (1, 8)), jnp.float32),
        "inverse_second": scatter_about(keys[7], (BOXES_X, BOXES_Y, SKEL, SKEL // 2), (SKEL * 5 // 4) ** -0.5, 0.25, ((0, 16), (1, 8)), jnp.float32),
        "inverse_third": scatter_about(keys[8], (BOXES_X, BOXES_Y, SKEL, SKEL // 4), (SKEL * 5 // 4) ** -0.5, 0.25, ((0, 16), (1, 8)), jnp.float32),
        "inverse_fourth": scatter_about(keys[9], (BOXES_X, BOXES_Y, SKEL, SKEL // 8), (SKEL * 5 // 4) ** -0.5, 0.25, ((0, 16), (1, 8)), jnp.float32),
        "couple_first": scatter_about(keys[10], (BOXES_X, BOXES_Y, 5, SKEL, SKEL), (10 * SKEL) ** -0.5, 0.09375, ((0, 16), (1, 8)), jnp.float32),
        "couple_second": scatter_about(keys[11], (BOXES_X, BOXES_Y, 5, SKEL, SKEL // 2), (10 * SKEL) ** -0.5, 0.09375, ((0, 16), (1, 8)), jnp.float32),
        "couple_third": scatter_about(keys[12], (BOXES_X, BOXES_Y, 5, SKEL, SKEL // 4), (10 * SKEL) ** -0.5, 0.09375, ((0, 16), (1, 8)), jnp.float32),
        "couple_fourth": scatter_about(keys[13], (BOXES_X, BOXES_Y, 5, SKEL, SKEL // 8), (10 * SKEL) ** -0.5, 0.09375, ((0, 16), (1, 8)), jnp.float32),
        "root_inverse": scatter_about(keys[14], (BOXES_X, BOXES_Y, SKEL, SKEL // 8), (2 * SKEL) ** -0.5, 0.21875, ((0, 16), (1, 8)), jnp.float32),
    }


HIGHEST = lax.Precision.HIGHEST
GROUPS = ((1, 1), (1, 2), (2, 2), (2, 4))
MERGE_ALONG = (1, 0, 1)


def assemble(pieces, level_index):
    if level_index == 0:
        return pieces
    total_x = pieces.shape[0]
    total_y = pieces.shape[1]
    inner_shape = tuple(pieces.shape[2:-1])
    piece_width = pieces.shape[-1]
    inner_rank = len(inner_shape)
    middle = list(range(inner_rank))
    if level_index == 1:
        blocks = pieces.reshape((total_x, total_y // 2, 2) + inner_shape + (piece_width,))
        axes_order = [0, 1] + [3 + position for position in middle] + [2, 3 + inner_rank]
        shape_out = (total_x, total_y // 2)
    elif level_index == 2:
        blocks = pieces.reshape((total_x // 2, 2, total_y // 2, 2) + inner_shape + (piece_width,))
        axes_order = [0, 2] + [4 + position for position in middle] + [1, 3, 4 + inner_rank]
        shape_out = (total_x // 2, total_y // 2)
    else:
        blocks = pieces.reshape((total_x // 2, 2, total_y // 4, 2, 2) + inner_shape + (piece_width,))
        axes_order = [0, 2] + [5 + position for position in middle] + [3, 1, 4, 5 + inner_rank]
        shape_out = (total_x // 2, total_y // 4)
    arranged = jnp.transpose(blocks, axes_order)
    return arranged.reshape(shape_out + inner_shape + (piece_width * 2 ** level_index,))


def from_lower(field, axis_number):
    padding = jnp.zeros_like(lax.slice_in_dim(field, 0, 1, axis=axis_number))
    kept = lax.slice_in_dim(field, 0, field.shape[axis_number] - 1, axis=axis_number)
    return jnp.concatenate([padding, kept], axis=axis_number)


def from_upper(field, axis_number):
    padding = jnp.zeros_like(lax.slice_in_dim(field, 0, 1, axis=axis_number))
    kept = lax.slice_in_dim(field, 1, field.shape[axis_number], axis=axis_number)
    return jnp.concatenate([kept, padding], axis=axis_number)


def reference(right_sides, skeleton_order, interp_first, interp_second, interp_third, interp_fourth,
              inverse_first, inverse_second, inverse_third, inverse_fourth,
              couple_first, couple_second, couple_third, couple_fourth, root_inverse):
    interps = (interp_first, interp_second, interp_third, interp_fourth)
    inverses = (inverse_first, inverse_second, inverse_third, inverse_fourth)
    couples = (couple_first, couple_second, couple_third, couple_fourth)
    vector = right_sides
    stored = []
    skeleton = vector
    for level_index in range(4):
        group_x, group_y = GROUPS[level_index]
        perm_grid = skeleton_order[::group_x, ::group_y, level_index]
        arranged = jnp.take_along_axis(vector, perm_grid[:, :, None, :], axis=3)
        skel_part = arranged[..., :SKEL]
        redund_part = arranged[..., SKEL:]
        interp_full = assemble(interps[level_index], level_index)
        inverse_full = assemble(inverses[level_index], level_index)
        couple_full = assemble(couples[level_index], level_index)
        lowered = redund_part - jnp.einsum("abns,absr->abnr", skel_part, interp_full, precision=HIGHEST)
        solved = jnp.einsum("abnk,abkr->abnr", lowered, inverse_full, precision=HIGHEST)
        stacked = jnp.stack([solved, from_lower(solved, 0), from_upper(solved, 0),
                             from_lower(solved, 1), from_upper(solved, 1)], axis=2)
        skeleton = skel_part - jnp.einsum("abknr,abkrs->abns", stacked, couple_full, precision=HIGHEST)
        stored.append((perm_grid, interp_full, inverse_full, couple_full, solved))
        if level_index < 3:
            if MERGE_ALONG[level_index] == 1:
                vector = jnp.concatenate([skeleton[:, 0::2], skeleton[:, 1::2]], axis=-1)
            else:
                vector = jnp.concatenate([skeleton[0::2], skeleton[1::2]], axis=-1)
    skel_value = jnp.einsum("abns,abst->abnt", skeleton, assemble(root_inverse, 3), precision=HIGHEST)
    for level_index in (3, 2, 1, 0):
        perm_grid, interp_full, inverse_full, couple_full, solved = stored[level_index]
        products = jnp.einsum("abns,abkrs->abknr", skel_value, couple_full, precision=HIGHEST)
        update = (products[:, :, 0] + from_upper(products[:, :, 1], 0) + from_lower(products[:, :, 2], 0)
                  + from_upper(products[:, :, 3], 1) + from_lower(products[:, :, 4], 1))
        redund_sol = solved - jnp.einsum("abnk,abrk->abnr", update, inverse_full, precision=HIGHEST)
        skel_sol = skel_value - jnp.einsum("abnr,absr->abns", redund_sol, interp_full, precision=HIGHEST)
        combined = jnp.concatenate([skel_sol, redund_sol], axis=-1)
        inverse_perm = jnp.argsort(perm_grid, axis=-1).astype(jnp.int32)
        vector = jnp.take_along_axis(combined, inverse_perm[:, :, None, :], axis=3)
        if level_index > 0:
            lower_half = vector[..., :SKEL]
            upper_half = vector[..., SKEL:]
            count_x, count_y, rows_count = vector.shape[0], vector.shape[1], vector.shape[2]
            if MERGE_ALONG[level_index - 1] == 1:
                skel_value = jnp.stack([lower_half, upper_half], axis=2).reshape(count_x, 2 * count_y, rows_count, SKEL)
            else:
                skel_value = jnp.stack([lower_half, upper_half], axis=1).reshape(2 * count_x, count_y, rows_count, SKEL)
    return vector
```

```python
import functools

import jax
import jax.numpy as jnp
from jax import lax
from jax.experimental import pallas as pl
from jax.experimental.pallas import tpu as pltpu
from jax.sharding import PartitionSpec as P

F32 = jnp.float32
BF16 = jnp.bfloat16
AXES = ("bx", "by")
S = 384
NN = (((1,), (0,)), ((), ()))
NT = (((1,), (1,)), ((), ()))
SHIFT_X = (0, 0, 1, 1)
SHIFT_Y = (0, 1, 1, 2)


def split(x):
    hi = x.astype(BF16)
    return hi, (x - hi.astype(F32)).astype(BF16)


def mm(a, bh, bl, dims):
    rows = a.shape[0]
    ah, al = split(a)
    both = lax.dot_general(jnp.concatenate([ah, al], 0), bh, dims, preferred_element_type=F32)
    low = lax.dot_general(ah, bl, dims, preferred_element_type=F32)
    return both[:rows] + (both[rows:] + low)


def select(a, hot, dims):
    rows = a.shape[0]
    ah, al = split(a)
    both = lax.dot_general(jnp.concatenate([ah, al], 0), hot, dims, preferred_element_type=F32)
    return both[:rows] + both[rows:]


def bits():
    i, j = lax.axis_index("bx"), lax.axis_index("by")
    return j & 1, i & 1, (j >> 1) & 1


def sides(level):
    px = (lax.axis_index("bx") >> SHIFT_X[level]) & 1
    py = (lax.axis_index("by") >> SHIFT_Y[level]) & 1
    if level == 3:
        return 2 - px, 1 + px, 3
    return 2 - px, 1 + px, 4 - py, 3 + py


def call(body, outs, *args, fetch=(), scratch=(), room=16, flops=50_000_000, size=3_000_000):
    vmem, far = pl.BlockSpec(memory_space=pltpu.VMEM), pl.BlockSpec(memory_space=pltpu.HBM)
    n_in, n_out, n_own = len(args), len(outs), len(scratch)

    def kernel(*refs):
        ins = list(refs[:n_in])
        rest = refs[n_in : n_in + n_out + n_own]
        staged = refs[n_in + n_out + n_own :]
        if fetch:
            sems = staged[-1]
            copies = []
            for n, (at, buf) in enumerate(zip(fetch, staged)):
                copies.append(pltpu.make_async_copy(ins[at], buf, sems.at[n]))
                copies[-1].start()
                ins[at] = buf
            for copy in copies:
                copy.wait()
        body(*ins, *rest)

    own = [pltpu.VMEM(sh, d) for sh, d in scratch]
    own += [pltpu.VMEM(args[at].shape, args[at].dtype) for at in fetch]
    if fetch:
        own.append(pltpu.SemaphoreType.DMA((len(fetch),)))
    return pl.pallas_call(
        kernel,
        out_shape=[jax.ShapeDtypeStruct(s, d) for s, d in outs],
        in_specs=[far if n in fetch else vmem for n in range(n_in)],
        out_specs=[vmem] * n_out,
        scratch_shapes=own,
        compiler_params=pltpu.CompilerParams(vmem_limit_bytes=room << 20),
        cost_estimate=pl.CostEstimate(flops=flops, bytes_accessed=size, transcendentals=0),
    )(*args)


def one_hot(order_ref, level):
    order = order_ref[level : level + 1, :]
    return (lax.broadcasted_iota(jnp.int32, (2 * S, 2 * S), 0) == order).astype(F32).astype(BF16)


def prep0_kernel(t_ref, g_ref, k_ref, ord_ref, tgh, tgl, kh, kl, hot):
    for n, ref in enumerate((t_ref, g_ref)):
        tgh[n], tgl[n] = split(ref[...])
    for n in range(5):
        kh[n], kl[n] = split(k_ref[n])
    hot[...] = one_hot(ord_ref, 0)


def pack_kernel(i2, n2, c2, i3, n3, r3, c3, w2, w3):
    far = 4 - ((lax.axis_index("by") >> SHIFT_Y[3]) & 1)
    for n, ref in enumerate((i2, n2)):
        w2[n] = ref[...]
    w2[2:] = c2[...]
    for n, ref in enumerate((i3, n3, r3)):
        w3[n] = ref[...]
    w3[3:6] = c3[:3]
    w3[6] = c3[far]


def pack(*arrays):
    outs = [((7, S >> l, S), F32) for l in (2, 3)]
    return call(pack_kernel, outs, *arrays, fetch=tuple(range(7)), room=60, flops=1000)


def prep_kernel(level, layout, *refs):
    n_in = 1 + max(n for _, blocks in layout for n, _ in blocks)
    ins, ord_ref = refs[:n_in], refs[n_in]
    tgh, tgl, kh, kl, hot = refs[n_in + 1 :]
    width = S >> level
    b = bits()
    piece = b[0] + 2 * b[1] * (level > 1) + 4 * b[2] * (level > 2)
    lead = tgh.shape[0]
    for place, blocks in layout:
        where = pl.ds(pl.multiple_of(place(piece) * width, width), width)
        for m, (n, index) in enumerate(blocks):
            hi, lo = split(ins[n][index])
            if m < lead:
                tgh[m, where, :], tgl[m, where, :] = hi, lo
            else:
                kh[m - lead, where, :], kl[m - lead, where, :] = hi, lo
    hot[...] = one_hot(ord_ref, level)


def prep(level, layout, pieces, orders):
    lead, coup = (3, 4) if level == 3 else (2, 5)
    outs = [((lead, S, S), BF16)] * 2 + [((coup, S, S), BF16)] * 2 + [((2 * S, 2 * S), BF16)]
    body = functools.partial(prep_kernel, level, layout)
    return call(body, outs, *pieces, orders, fetch=tuple(range(len(pieces))))


def first_kernel(v_ref, ord_ref, t_ref, g_ref, s_ref, y_ref):
    a = select(v_ref[...], one_hot(ord_ref, 0), NN)
    s0 = a[:, :S]
    w = a[:, S:] - mm(s0, *split(t_ref[...]), NN)
    s_ref[...] = s0
    y_ref[...] = mm(w, *split(g_ref[...]), NN)


def reduce_kernel(level, own_ref, got_ref, hot, tgh, tgl, s_ref, y_ref):
    b = bits()[level - 1]
    own, got = own_ref[...], got_ref[...]
    lower = jnp.where(b == 0, own, got)
    upper = jnp.where(b == 0, got, own)
    a = select(lower, hot[:S, :], NN) + select(upper, hot[S:, :], NN)
    s0 = a[:, :S]
    w = a[:, S:] - mm(s0, tgh[0], tgl[0], NT)
    s_ref[...] = s0
    y_ref[...] = mm(w, tgh[1], tgl[1], NT)


def own_kernel(dims, s_ref, y_ref, kh, kl, o_ref):
    o_ref[...] = s_ref[...] - mm(y_ref[...], kh[0], kl[0], dims)


def couple(level, acc, got, kh, kl, dims):
    for ref, k in zip(got, sides(level)):
        acc = acc - mm(ref[...], kh[k], kl[k], dims)
    return acc


def couple0_kernel(acc_ref, g0, g1, g2, g3, kh, kl, keep_ref, send_ref, full):
    full[...] = couple(0, acc_ref[...], (g0, g1, g2, g3), kh, kl, NN)
    b = bits()[0]
    keep_ref[...] = full[pl.ds(pl.multiple_of(b * 64, 64), 64), :]
    send_ref[...] = full[pl.ds(pl.multiple_of((1 - b) * 64, 64), 64), :]


def couple_kernel(level, acc_ref, g0, g1, g2, g3, kh, kl, o_ref):
    o_ref[...] = couple(level, acc_ref[...], (g0, g1, g2, g3), kh, kl, NT)


def root_kernel(acc_ref, g0, g1, g2, kh, kl, tgh, tgl, t_ref, *q_refs):
    skeleton = couple(3, acc_ref[...], (g0, g1, g2), kh, kl, NT)
    t = mm(skeleton, tgh[2], tgl[2], NT)
    t_ref[...] = t
    spread(3, t, kh, kl, q_refs, NN)


def spread(level, t, kh, kl, q_refs, dims):
    for ref, k in zip(q_refs, sides(level)):
        ref[...] = mm(t, kh[k], kl[k], dims)


def own_back_kernel(dims, t_ref, kh, kl, o_ref):
    o_ref[...] = mm(t_ref[...], kh[0], kl[0], dims)


def solve(t, y, q0, got, tgh, tgl, dims):
    u = q0
    for ref in got:
        u = u + ref[...]
    xr = y - mm(u, tgh[1], tgl[1], dims)
    xs = t - mm(xr, tgh[0], tgl[0], dims)
    return jnp.concatenate([xs, xr], 1)


def down_kernel(level, n_got, *refs):
    t_ref, y_ref, q0_ref = refs[:3]
    got = refs[3 : 3 + n_got]
    tgh, tgl, hot, kh, kl, o_ref, *q_refs = refs[3 + n_got :]
    both = solve(t_ref[...], y_ref[...], q0_ref[...], got, tgh, tgl, NN)
    b = bits()[level - 1]
    half = hot[pl.ds(pl.multiple_of(b * S, S), S), :]
    t = select(both, half, NT)
    o_ref[...] = t
    spread(level - 1, t, kh, kl, q_refs, NN)


def down1_kernel(t_ref, y_ref, q0_ref, g0, g1, g2, g3, tgh, tgl, hot, keep_ref, send_ref):
    both = solve(t_ref[...], y_ref[...], q0_ref[...], (g0, g1, g2, g3), tgh, tgl, NN)
    b = bits()[0]
    send_ref[...] = select(both, hot[pl.ds(pl.multiple_of((1 - b) * S, S), S), :], NT)
    keep_ref[...] = select(both, hot[pl.ds(pl.multiple_of(b * S, S), S), :], NT)


def spread0_kernel(keep_ref, got_ref, kh, kl, t_ref, *q_refs):
    b = bits()[0]
    keep, got = keep_ref[...], got_ref[...]
    t = jnp.concatenate([jnp.where(b == 0, keep, got), jnp.where(b == 0, got, keep)], 0)
    t_ref[...] = t
    spread(0, t, kh, kl, q_refs, NT)


def last_kernel(t_ref, y_ref, q0_ref, g0, g1, g2, g3, tgh, tgl, hot, o_ref):
    both = solve(t_ref[...], y_ref[...], q0_ref[...], (g0, g1, g2, g3), tgh, tgl, NT)
    o_ref[...] = select(both, hot[...], NT)


def paired(x, axis, distance, odd):
    n = lax.axis_size(axis)
    shift = distance if odd else 0
    route = [(i, ((i + shift) ^ distance) - shift) for i in range(n)]
    return lax.ppermute(x, axis, [(i, k) for i, k in route if 0 <= k < n])


def halo(level, fields):
    dx, dy = 1 << SHIFT_X[level], 1 << SHIFT_Y[level]
    if level == 3:
        return [
            paired(fields[0], "bx", dx, False),
            paired(fields[1], "bx", dx, True),
            paired(fields[2], "by", dy, False),
        ]
    return [
        paired(fields[0], "bx", dx, False),
        paired(fields[1], "bx", dx, True),
        paired(fields[2], "by", dy, False),
        paired(fields[3], "by", dy, True),
    ]


def core_swap(x):
    return paired(x, "by", 1, False)


def x_swap(x):
    return paired(x, "bx", 1, False)


def z_swap(x):
    return paired(x, "by", 2, False)


def gather_pairs(x, axis, distance):
    n = lax.axis_size(axis)
    groups = [[i, i ^ distance] for i in range(n) if i < i ^ distance]
    return lax.all_gather(x, axis, axis_index_groups=groups)


def after(x, event):
    return lax.optimization_barrier((x, event))[0]


def masked(mask):
    return lambda piece: piece ^ mask


def body(rhs, order, i0, i1, i2, i3, n0, n1, n2, n3, c0, c1, c2, c3, root):
    orders = order[0, 0]
    turned = lambda x: jnp.swapaxes(x[0, 0], -1, -2)
    own1 = [turned(x) for x in (i1, n1, c1)]
    w2, w3 = pack(*[turned(x) for x in (i2, n2, c2, i3, n3, root, c3)])
    z3 = gather_pairs(w3, "by", 2)

    m, h = (128, S), (64, S)
    s0, y0 = call(
        first_kernel, [(m, F32)] * 2, after(rhs[0, 0], w2), orders, i0[0, 0], n0[0, 0],
        fetch=(0, 1, 2, 3), room=59,
    )
    got = halo(0, [y0] * 4)
    tgh0, tgl0, kh0, kl0, hot0 = call(
        prep0_kernel,
        [((2, S, S), BF16)] * 2 + [((5, S, S), BF16)] * 2 + [((2 * S, 2 * S), BF16)],
        i0[0, 0], n0[0, 0], c0[0, 0], after(orders, y0),
        fetch=(0, 1, 2, 3),
    )
    (acc,) = call(functools.partial(own_kernel, NN), [(m, F32)], s0, y0, kh0, kl0)
    keep, send = call(couple0_kernel, [(h, F32)] * 2, acc, *got, kh0, kl0, scratch=[(m, F32)])
    far1 = [core_swap(after(x, y0)) for x in own1]
    x2 = x_swap(after(w2, got))
    w2c = core_swap(after(w2, got))
    ready = {}
    spans = lambda n, lead: [(n + k, slice(None)) for k in range(lead)] + [(n + lead, k) for k in range(5)]
    ready[1] = prep(1, [(masked(0), spans(0, 2)), (masked(1), spans(3, 2))], own1 + far1, orders)

    kept = {0: y0}
    own, other = keep, core_swap(send)
    for level in (1, 2, 3):
        tgh, tgl, kh, kl, hot = ready[level]
        s, y = call(
            functools.partial(reduce_kernel, level), [(h, F32)] * 2, own, other, hot, tgh, tgl
        )
        kept[level] = y
        got = halo(level, [y] * 4)
        (acc,) = call(functools.partial(own_kernel, NT), [(h, F32)], s, y, kh, kl)
        if level == 1:
            x2 = after(x2, got)
            layout = [(masked(n), [(n, k) for k in range(7)]) for n in range(4)]
            ready[2] = prep(2, layout, [w2, w2c, x2, core_swap(x2)], orders)
        if level == 2:
            x3 = x_swap(after(w3, other))
            zx3 = z_swap(after(x3, acc))
            near = [after(z3, got), x3, zx3]
            far = [core_swap(after(v, got)) for v in near]
            layout = []
            at_z = lambda c, at, piece: (piece & 3 ^ c) + 4 * at
            for c in (0, 1):
                for at in (0, 1):
                    layout.append((functools.partial(at_z, c, at), [(3 * c, (at, k)) for k in range(7)]))
                layout.append((masked(2 + c), [(1 + 3 * c, k) for k in range(7)]))
                layout.append((masked(6 + c), [(2 + 3 * c, k) for k in range(7)]))
            ready[3] = prep(3, layout, near + far, orders)
        if level < 3:
            (own,) = call(functools.partial(couple_kernel, level), [(h, F32)], acc, *got, kh, kl)
            other = x_swap(own) if level == 1 else z_swap(own)
    t, *q = call(root_kernel, [(h, F32)] * 4, acc, *got, kh, kl, tgh, tgl)
    for level in (3, 2):
        tgh, tgl, kh, kl, hot = ready[level]
        got = halo(level, q)
        (q0,) = call(functools.partial(own_back_kernel, NN), [(h, F32)], t, kh, kl)
        t, *q = call(
            functools.partial(down_kernel, level, len(got)),
            [(h, F32)] * 5,
            t, kept[level], q0, *got, tgh, tgl, hot, ready[level - 1][2], ready[level - 1][3],
        )
    tgh, tgl, kh, kl, hot = ready[1]
    got = halo(1, q)
    (q0,) = call(functools.partial(own_back_kernel, NN), [(h, F32)], t, kh, kl)
    keep, send = call(down1_kernel, [(h, F32)] * 2, t, kept[1], q0, *got, tgh, tgl, hot)
    t, *q = call(spread0_kernel, [(m, F32)] * 5, keep, core_swap(send), kh0, kl0)
    got = halo(0, q)
    (q0,) = call(functools.partial(own_back_kernel, NT), [(m, F32)], t, kh0, kl0)
    (x,) = call(last_kernel, [((128, 2 * S), F32)], t, kept[0], q0, *got, tgh0, tgl0, hot0)
    return x[None, None]


def solution(mesh):
    four = P("bx", "by", None, None)
    five = P("bx", "by", None, None, None)
    in_specs = (four,) * 10 + (five,) * 4 + (four,)
    return jax.shard_map(body, mesh=mesh, in_specs=in_specs, out_specs=four, check_vma=False)
```

```python
import functools

import jax
import jax.numpy as jnp
from jax import lax
from jax.experimental import pallas as pl
from jax.experimental.pallas import tpu as pltpu
from jax.sharding import PartitionSpec as P

F32 = jnp.float32
BF16 = jnp.bfloat16
AXES = ("bx", "by")
S = 384
NN = (((1,), (0,)), ((), ()))
NT = (((1,), (1,)), ((), ()))
SHIFT_X = (0, 0, 1, 1)
SHIFT_Y = (0, 1, 1, 2)


def split(x):
    hi = x.astype(BF16)
    return hi, (x - hi.astype(F32)).astype(BF16)


def mm(a, bh, bl, dims):
    rows = a.shape[0]
    ah, al = split(a)
    both = lax.dot_general(jnp.concatenate([ah, al], 0), bh, dims, preferred_element_type=F32)
    low = lax.dot_general(ah, bl, dims, preferred_element_type=F32)
    return both[:rows] + (both[rows:] + low)


def select(a, hot, dims):
    rows = a.shape[0]
    ah, al = split(a)
    both = lax.dot_general(jnp.concatenate([ah, al], 0), hot, dims, preferred_element_type=F32)
    return both[:rows] + both[rows:]


def bits():
    i, j = lax.axis_index("bx"), lax.axis_index("by")
    return j & 1, i & 1, (j >> 1) & 1


def sides(level):
    px = (lax.axis_index("bx") >> SHIFT_X[level]) & 1
    py = (lax.axis_index("by") >> SHIFT_Y[level]) & 1
    if level == 3:
        return 2 - px, 1 + px, 3
    return 2 - px, 1 + px, 4 - py, 3 + py


def call(body, outs, *args, fetch=(), scratch=(), room=16, flops=50_000_000, size=3_000_000):
    vmem, far = pl.BlockSpec(memory_space=pltpu.VMEM), pl.BlockSpec(memory_space=pltpu.HBM)
    n_in, n_out, n_own = len(args), len(outs), len(scratch)

    def kernel(*refs):
        ins = list(refs[:n_in])
        rest = refs[n_in : n_in + n_out + n_own]
        staged = refs[n_in + n_out + n_own :]
        if fetch:
            sems = staged[-1]
            copies = []
            for n, (at, buf) in enumerate(zip(fetch, staged)):
                copies.append(pltpu.make_async_copy(ins[at], buf, sems.at[n]))
                copies[-1].start()
                ins[at] = buf
            for copy in copies:
                copy.wait()
        body(*ins, *rest)

    own = [pltpu.VMEM(sh, d) for sh, d in scratch]
    own += [pltpu.VMEM(args[at].shape, args[at].dtype) for at in fetch]
    if fetch:
        own.append(pltpu.SemaphoreType.DMA((len(fetch),)))
    return pl.pallas_call(
        kernel,
        out_shape=[jax.ShapeDtypeStruct(s, d) for s, d in outs],
        in_specs=[far if n in fetch else vmem for n in range(n_in)],
        out_specs=[vmem] * n_out,
        scratch_shapes=own,
        compiler_params=pltpu.CompilerParams(vmem_limit_bytes=room << 20),
        cost_estimate=pl.CostEstimate(flops=flops, bytes_accessed=size, transcendentals=0),
    )(*args)


def one_hot(order_ref, level):
    order = order_ref[level : level + 1, :]
    return (lax.broadcasted_iota(jnp.int32, (2 * S, 2 * S), 0) == order).astype(F32).astype(BF16)


def prep0_kernel(t_ref, g_ref, k_ref, ord_ref, tgh, tgl, kh, kl, hot):
    for n, ref in enumerate((t_ref, g_ref)):
        tgh[n], tgl[n] = split(ref[...])
    for n in range(5):
        kh[n], kl[n] = split(k_ref[n])
    hot[...] = one_hot(ord_ref, 0)


ROWS = tuple(7 * (S >> level) for level in range(4))


def lay(out, row, blocks):
    for block in blocks:
        out[row : row + block.shape[0], :] = block
        row += block.shape[0]


def pack3_kernel(i3, n3, r3, c3, w3):
    far = 4 - ((lax.axis_index("by") >> SHIFT_Y[3]) & 1)
    lay(w3, 0, [i3[...], n3[...], r3[...]] + [c3[k] for k in range(3)] + [c3[far]])


def pack12_kernel(i1, n1, c1, i2, n2, c2, w12, lead2, coup2):
    lay(w12, 0, [i1[...], n1[...]] + [c1[k] for k in range(5)])
    lead, coup = [i2[...], n2[...]], [c2[k] for k in range(5)]
    lay(w12, ROWS[1], lead + coup)
    lay(lead2, 0, lead)
    lay(coup2, 0, coup)


def pack3(*arrays):
    return call(pack3_kernel, [((ROWS[3], S), F32)], *arrays, fetch=(0, 1, 2, 3), room=60, flops=1000)[0]


def pack12(*arrays):
    outs = [((rows, S), F32) for rows in (ROWS[1] + ROWS[2], 2 * (S >> 2), 5 * (S >> 2))]
    return call(pack12_kernel, outs, *arrays, fetch=tuple(range(6)), room=56, flops=1000)


def prep_kernel(level, places, base, count, hot_too, *refs):
    n_in = len(places)
    ins, ord_ref, (high, low, *hot) = refs[:n_in], refs[n_in], refs[n_in + 1 : n_in + 3 + hot_too]
    bufs, sems = refs[n_in + 3 + hot_too : -1], refs[-1]
    width = S >> level
    copies = [
        pltpu.make_async_copy(ref.at[pl.ds(row, count * width)], buf, sems.at[n])
        for n, (ref, buf, row) in enumerate(zip(ins, bufs, base))
    ]
    for copy in copies:
        copy.start()
    if hot_too:
        hot[0][...] = one_hot(ord_ref, level)
    b = bits()
    piece = b[0] + 2 * b[1] * (level > 1) + 4 * b[2] * (level > 2)
    for n, mask in enumerate(places):
        copies[n].wait()
        where = pl.ds(pl.multiple_of((piece ^ mask) * width, width), width)
        for m in range(count):
            hi, lo = split(bufs[n][m * width : (m + 1) * width, :])
            high[m, where, :], low[m, where, :] = hi, lo


def prep_part(level, pieces, first, count, orders, hot_too):
    width = S >> level
    arrays = [x for _, x, _ in pieces]
    base = [row + first * width for _, _, row in pieces]
    outs = [((count, S, S), BF16)] * 2 + [((2 * S, 2 * S), BF16)] * hot_too
    vmem, far = pl.BlockSpec(memory_space=pltpu.VMEM), pl.BlockSpec(memory_space=pltpu.HBM)
    places = [mask for mask, _, _ in pieces]
    return pl.pallas_call(
        functools.partial(prep_kernel, level, places, base, count, hot_too),
        out_shape=[jax.ShapeDtypeStruct(sh, d) for sh, d in outs],
        in_specs=[far] * len(arrays) + [vmem],
        out_specs=[vmem] * len(outs),
        scratch_shapes=[pltpu.VMEM((count * width, S), F32)] * len(arrays)
        + [pltpu.SemaphoreType.DMA((len(arrays),))],
        compiler_params=pltpu.CompilerParams(vmem_limit_bytes=16 << 20),
        cost_estimate=pl.CostEstimate(flops=1000, bytes_accessed=3_000_000, transcendentals=0),
    )(*arrays, orders)


def prep(level, leads, coups, orders):
    lead = 3 if level == 3 else 2
    tgh, tgl, hot = prep_part(level, leads, 0, lead, orders, True)
    kh, kl = prep_part(level, coups, lead, 7 - lead, orders, False)
    return tgh, tgl, kh, kl, hot


def first_kernel(v_ref, ord_ref, t_ref, g_ref, s_ref, y_ref):
    a = select(v_ref[...], one_hot(ord_ref, 0), NN)
    s0 = a[:, :S]
    w = a[:, S:] - mm(s0, *split(t_ref[...]), NN)
    s_ref[...] = s0
    y_ref[...] = mm(w, *split(g_ref[...]), NN)


def reduce_kernel(level, own_ref, got_ref, hot, tgh, tgl, s_ref, y_ref):
    b = bits()[level - 1]
    own, got = own_ref[...], got_ref[...]
    lower = jnp.where(b == 0, own, got)
    upper = jnp.where(b == 0, got, own)
    a = select(lower, hot[:S, :], NN) + select(upper, hot[S:, :], NN)
    s0 = a[:, :S]
    w = a[:, S:] - mm(s0, tgh[0], tgl[0], NT)
    s_ref[...] = s0
    y_ref[...] = mm(w, tgh[1], tgl[1], NT)


def own_kernel(dims, s_ref, y_ref, kh, kl, o_ref):
    o_ref[...] = s_ref[...] - mm(y_ref[...], kh[0], kl[0], dims)


def couple(level, acc, got, kh, kl, dims):
    for ref, k in zip(got, sides(level)):
        acc = acc - mm(ref[...], kh[k], kl[k], dims)
    return acc


def couple0_kernel(acc_ref, g0, g1, g2, g3, kh, kl, keep_ref, send_ref, full):
    full[...] = couple(0, acc_ref[...], (g0, g1, g2, g3), kh, kl, NN)
    b = bits()[0]
    keep_ref[...] = full[pl.ds(pl.multiple_of(b * 64, 64), 64), :]
    send_ref[...] = full[pl.ds(pl.multiple_of((1 - b) * 64, 64), 64), :]


def couple_kernel(level, acc_ref, g0, g1, g2, g3, kh, kl, o_ref):
    o_ref[...] = couple(level, acc_ref[...], (g0, g1, g2, g3), kh, kl, NT)


def root_kernel(acc_ref, g0, g1, g2, kh, kl, tgh, tgl, t_ref, *q_refs):
    skeleton = couple(3, acc_ref[...], (g0, g1, g2), kh, kl, NT)
    t = mm(skeleton, tgh[2], tgl[2], NT)
    t_ref[...] = t
    spread(3, t, kh, kl, q_refs, NN)


def spread(level, t, kh, kl, q_refs, dims):
    for ref, k in zip(q_refs, sides(level)):
        ref[...] = mm(t, kh[k], kl[k], dims)


def own_back_kernel(dims, t_ref, kh, kl, o_ref):
    o_ref[...] = mm(t_ref[...], kh[0], kl[0], dims)


def solve(t, y, q0, got, tgh, tgl, dims):
    u = q0
    for ref in got:
        u = u + ref[...]
    xr = y - mm(u, tgh[1], tgl[1], dims)
    xs = t - mm(xr, tgh[0], tgl[0], dims)
    return jnp.concatenate([xs, xr], 1)


def down_kernel(level, n_got, *refs):
    t_ref, y_ref, q0_ref = refs[:3]
    got = refs[3 : 3 + n_got]
    tgh, tgl, hot, kh, kl, o_ref, *q_refs = refs[3 + n_got :]
    both = solve(t_ref[...], y_ref[...], q0_ref[...], got, tgh, tgl, NN)
    b = bits()[level - 1]
    half = hot[pl.ds(pl.multiple_of(b * S, S), S), :]
    t = select(both, half, NT)
    o_ref[...] = t
    spread(level - 1, t, kh, kl, q_refs, NN)


def down1_kernel(t_ref, y_ref, q0_ref, g0, g1, g2, g3, tgh, tgl, hot, keep_ref, send_ref):
    both = solve(t_ref[...], y_ref[...], q0_ref[...], (g0, g1, g2, g3), tgh, tgl, NN)
    b = bits()[0]
    send_ref[...] = select(both, hot[pl.ds(pl.multiple_of((1 - b) * S, S), S), :], NT)
    keep_ref[...] = select(both, hot[pl.ds(pl.multiple_of(b * S, S), S), :], NT)


def spread0_kernel(keep_ref, got_ref, kh, kl, t_ref, *q_refs):
    b = bits()[0]
    keep, got = keep_ref[...], got_ref[...]
    t = jnp.concatenate([jnp.where(b == 0, keep, got), jnp.where(b == 0, got, keep)], 0)
    t_ref[...] = t
    spread(0, t, kh, kl, q_refs, NT)


def last_kernel(t_ref, y_ref, q0_ref, g0, g1, g2, g3, tgh, tgl, hot, o_ref):
    both = solve(t_ref[...], y_ref[...], q0_ref[...], (g0, g1, g2, g3), tgh, tgl, NT)
    o_ref[...] = select(both, hot[...], NT)


def paired(x, axis, distance, odd):
    n = lax.axis_size(axis)
    shift = distance if odd else 0
    route = [(i, ((i + shift) ^ distance) - shift) for i in range(n)]
    return lax.ppermute(x, axis, [(i, k) for i, k in route if 0 <= k < n])


def halo(level, fields):
    dx, dy = 1 << SHIFT_X[level], 1 << SHIFT_Y[level]
    if level == 3:
        return [
            paired(fields[0], "bx", dx, False),
            paired(fields[1], "bx", dx, True),
            paired(fields[2], "by", dy, False),
        ]
    return [
        paired(fields[0], "bx", dx, False),
        paired(fields[1], "bx", dx, True),
        paired(fields[2], "by", dy, False),
        paired(fields[3], "by", dy, True),
    ]


def core_swap(x):
    return paired(x, "by", 1, False)


def x_swap(x):
    return paired(x, "bx", 1, False)


def z_swap(x):
    return paired(x, "by", 2, False)


def gather_pairs(x, axis, distance):
    n = lax.axis_size(axis)
    groups = [[i, i ^ distance] for i in range(n) if i < i ^ distance]
    return lax.all_gather(x, axis, axis_index_groups=groups)


def after(x, event):
    return lax.optimization_barrier((x, event))[0]


def masked(mask):
    return lambda piece: piece ^ mask


def body(rhs, order, i0, i1, i2, i3, n0, n1, n2, n3, c0, c1, c2, c3, root):
    orders = order[0, 0]
    turned = lambda x: jnp.swapaxes(x[0, 0], -1, -2)
    w3 = pack3(*[turned(x) for x in (i3, n3, root, c3)])
    x3, z3 = x_swap(w3), z_swap(w3)

    m, h = (128, S), (64, S)
    s0, y0 = call(
        first_kernel, [(m, F32)] * 2, after(rhs[0, 0], w3), orders, i0[0, 0], n0[0, 0],
        fetch=(0, 1, 2, 3), room=59,
    )
    w12, lead2, coup2 = pack12(*[turned(x) for x in (after(i1, y0), n1, c1, i2, n2, c2)])
    y0, x3, z3, w12 = lax.optimization_barrier((y0, x3, z3, w12))
    c12 = core_swap(w12)
    got = halo(0, [y0] * 4)
    tgh0, tgl0, kh0, kl0, hot0 = call(
        prep0_kernel,
        [((2, S, S), BF16)] * 2 + [((5, S, S), BF16)] * 2 + [((2 * S, 2 * S), BF16)],
        i0[0, 0], n0[0, 0], c0[0, 0], after(orders, y0),
        fetch=(0, 1, 2, 3),
    )
    (acc,) = call(functools.partial(own_kernel, NN), [(m, F32)], s0, y0, kh0, kl0)
    keep, send = call(couple0_kernel, [(h, F32)] * 2, acc, *got, kh0, kl0, scratch=[(m, F32)])
    lead2x, zx3 = x_swap(after(lead2, got)), z_swap(after(x3, got))
    pieces = [(0, w12, 0), (1, c12, 0)]
    ready = {1: prep(1, pieces, pieces, orders)}

    kept = {0: y0}
    own, other = keep, core_swap(send)
    for level in (1, 2, 3):
        tgh, tgl, kh, kl, hot = ready[level]
        s, y = call(
            functools.partial(reduce_kernel, level), [(h, F32)] * 2, own, other, hot, tgh, tgl
        )
        if level == 1:
            lead2xc = core_swap(after(lead2x, y))
            y, lead2xc = lax.optimization_barrier((y, lead2xc))
        kept[level] = y
        if level == 2:
            coup2x = x_swap(after(coup2, other))
        got = halo(level, [y] * 4)
        if level == 2:
            first = -2 * (S >> 2)
            coups = near + [(2, coup2x, first), (3, core_swap(after(coup2x, got)), first)]
            kh, kl = prep_part(2, coups, 2, 5, orders, False)
            ready[2] = (tgh, tgl, kh, kl, hot)
        (acc,) = call(functools.partial(own_kernel, NT), [(h, F32)], s, y, kh, kl)
        if level == 1:
            near = [(0, w12, ROWS[1]), (1, c12, ROWS[1])]
            leads = near + [(2, lead2x, 0), (3, lead2xc, 0)]
            *lead_parts, hot2 = prep_part(2, leads, 0, 2, orders, True)
            ready[2] = (*lead_parts, None, None, hot2)
        if level == 2:
            pieces = [(2 * n, v, 0) for n, v in enumerate((w3, x3, z3, zx3))]
            pieces += [(m + 1, core_swap(after(v, got)), 0) for m, v, _ in pieces]
            ready[3] = prep(3, pieces, pieces, orders)
        if level < 3:
            (own,) = call(functools.partial(couple_kernel, level), [(h, F32)], acc, *got, kh, kl)
            if level == 1:
                own, zx3 = lax.optimization_barrier((own, zx3))
            other = x_swap(own) if level == 1 else z_swap(own)
    t, *q = call(root_kernel, [(h, F32)] * 4, acc, *got, kh, kl, tgh, tgl)
    for level in (3, 2):
        tgh, tgl, kh, kl, hot = ready[level]
        got = halo(level, q)
        (q0,) = call(functools.partial(own_back_kernel, NN), [(h, F32)], t, kh, kl)
        t, *q = call(
            functools.partial(down_kernel, level, len(got)),
            [(h, F32)] * 5,
            t, kept[level], q0, *got, tgh, tgl, hot, ready[level - 1][2], ready[level - 1][3],
        )
    tgh, tgl, kh, kl, hot = ready[1]
    got = halo(1, q)
    (q0,) = call(functools.partial(own_back_kernel, NN), [(h, F32)], t, kh, kl)
    keep, send = call(down1_kernel, [(h, F32)] * 2, t, kept[1], q0, *got, tgh, tgl, hot)
    t, *q = call(spread0_kernel, [(m, F32)] * 5, keep, core_swap(send), kh0, kl0)
    got = halo(0, q)
    (q0,) = call(functools.partial(own_back_kernel, NT), [(m, F32)], t, kh0, kl0)
    (x,) = call(last_kernel, [((128, 2 * S), F32)], t, kept[0], q0, *got, tgh0, tgl0, hot0)
    return x[None, None]


def solution(mesh):
    four = P("bx", "by", None, None)
    five = P("bx", "by", None, None, None)
    in_specs = (four,) * 10 + (five,) * 4 + (four,)
    return jax.shard_map(body, mesh=mesh, in_specs=in_specs, out_specs=four, check_vma=False)
```

```python
import functools

import jax
import jax.numpy as jnp
from jax import lax
from jax.experimental import pallas as pl
from jax.experimental.pallas import tpu as pltpu
from jax.sharding import PartitionSpec as P

F32 = jnp.float32
BF16 = jnp.bfloat16
AXES = ("bx", "by")
S = 384
NN = (((1,), (0,)), ((), ()))
NT = (((1,), (1,)), ((), ()))
SHIFT_X = (0, 0, 1, 1)
SHIFT_Y = (0, 1, 1, 2)


def split(x):
    hi = x.astype(BF16)
    return hi, (x - hi.astype(F32)).astype(BF16)


def mm(a, bh, bl, dims):
    rows = a.shape[0]
    ah, al = split(a)
    both = lax.dot_general(jnp.concatenate([ah, al], 0), bh, dims, preferred_element_type=F32)
    low = lax.dot_general(ah, bl, dims, preferred_element_type=F32)
    return both[:rows] + (both[rows:] + low)


def select(a, hot, dims):
    rows = a.shape[0]
    ah, al = split(a)
    both = lax.dot_general(jnp.concatenate([ah, al], 0), hot, dims, preferred_element_type=F32)
    return both[:rows] + both[rows:]


def bits():
    i, j = lax.axis_index("bx"), lax.axis_index("by")
    return j & 1, i & 1, (j >> 1) & 1


def sides(level):
    px = (lax.axis_index("bx") >> SHIFT_X[level]) & 1
    py = (lax.axis_index("by") >> SHIFT_Y[level]) & 1
    if level == 3:
        return 2 - px, 1 + px, 3
    return 2 - px, 1 + px, 4 - py, 3 + py


def call(body, outs, *args, fetch=(), scratch=(), room=16, flops=50_000_000, size=3_000_000):
    vmem, far = pl.BlockSpec(memory_space=pltpu.VMEM), pl.BlockSpec(memory_space=pltpu.HBM)
    n_in, n_out, n_own = len(args), len(outs), len(scratch)

    def kernel(*refs):
        ins = list(refs[:n_in])
        rest = refs[n_in : n_in + n_out + n_own]
        staged = refs[n_in + n_out + n_own :]
        if fetch:
            sems = staged[-1]
            copies = []
            for n, (at, buf) in enumerate(zip(fetch, staged)):
                copies.append(pltpu.make_async_copy(ins[at], buf, sems.at[n]))
                copies[-1].start()
                ins[at] = buf
            for copy in copies:
                copy.wait()
        body(*ins, *rest)

    own = [pltpu.VMEM(sh, d) for sh, d in scratch]
    own += [pltpu.VMEM(args[at].shape, args[at].dtype) for at in fetch]
    if fetch:
        own.append(pltpu.SemaphoreType.DMA((len(fetch),)))
    return pl.pallas_call(
        kernel,
        out_shape=[jax.ShapeDtypeStruct(s, d) for s, d in outs],
        in_specs=[far if n in fetch else vmem for n in range(n_in)],
        out_specs=[vmem] * n_out,
        scratch_shapes=own,
        compiler_params=pltpu.CompilerParams(vmem_limit_bytes=room << 20),
        cost_estimate=pl.CostEstimate(flops=flops, bytes_accessed=size, transcendentals=0),
    )(*args)


def one_hot(order_ref, level):
    order = order_ref[level : level + 1, :]
    return (lax.broadcasted_iota(jnp.int32, (2 * S, 2 * S), 0) == order).astype(F32).astype(BF16)


def prep0_kernel(t_ref, g_ref, k_ref, ord_ref, tgh, tgl, kh, kl, hot):
    for n, ref in enumerate((t_ref, g_ref)):
        tgh[n], tgl[n] = split(ref[...])
    for n in range(5):
        kh[n], kl[n] = split(k_ref[n])
    hot[...] = one_hot(ord_ref, 0)


ROWS = tuple(7 * (S >> level) for level in range(4))


def lay(out, row, blocks):
    for block in blocks:
        out[row : row + block.shape[0], :] = block
        row += block.shape[0]


def pack3_kernel(i3, n3, r3, c3, w3):
    far = 4 - ((lax.axis_index("by") >> SHIFT_Y[3]) & 1)
    lay(w3, 0, [i3[...], n3[...], r3[...]] + [c3[k] for k in range(3)] + [c3[far]])


def pack12_kernel(i1, n1, c1, i2, n2, c2, w12, lead2, coup2):
    lay(w12, 0, [i1[...], n1[...]] + [c1[k] for k in range(5)])
    lead, coup = [i2[...], n2[...]], [c2[k] for k in range(5)]
    lay(w12, ROWS[1], lead + coup)
    lay(lead2, 0, lead)
    lay(coup2, 0, coup)


def pack3(*arrays):
    return call(pack3_kernel, [((ROWS[3], S), F32)], *arrays, fetch=(0, 1, 2, 3), room=60, flops=1000)[0]


def pack12(*arrays):
    outs = [((rows, S), F32) for rows in (ROWS[1] + ROWS[2], 2 * (S >> 2), 5 * (S >> 2))]
    return call(pack12_kernel, outs, *arrays, fetch=tuple(range(6)), room=56, flops=1000)


def prep_kernel(level, places, base, count, hot_too, *refs):
    n_in = len(places)
    ins, ord_ref, (high, low, *hot) = refs[:n_in], refs[n_in], refs[n_in + 1 : n_in + 3 + hot_too]
    bufs, sems = refs[n_in + 3 + hot_too : -1], refs[-1]
    width = S >> level
    copies = [
        pltpu.make_async_copy(ref.at[pl.ds(row, count * width)], buf, sems.at[n])
        for n, (ref, buf, row) in enumerate(zip(ins, bufs, base))
    ]
    for copy in copies:
        copy.start()
    if hot_too:
        hot[0][...] = one_hot(ord_ref, level)
    b = bits()
    piece = b[0] + 2 * b[1] * (level > 1) + 4 * b[2] * (level > 2)
    for n, mask in enumerate(places):
        copies[n].wait()
        where = pl.ds(pl.multiple_of((piece ^ mask) * width, width), width)
        for m in range(count):
            hi, lo = split(bufs[n][m * width : (m + 1) * width, :])
            high[m, where, :], low[m, where, :] = hi, lo


def prep_part(level, pieces, first, count, orders, hot_too):
    width = S >> level
    arrays = [x for _, x, _ in pieces]
    base = [row + first * width for _, _, row in pieces]
    outs = [((count, S, S), BF16)] * 2 + [((2 * S, 2 * S), BF16)] * hot_too
    vmem, far = pl.BlockSpec(memory_space=pltpu.VMEM), pl.BlockSpec(memory_space=pltpu.HBM)
    places = [mask for mask, _, _ in pieces]
    return pl.pallas_call(
        functools.partial(prep_kernel, level, places, base, count, hot_too),
        out_shape=[jax.ShapeDtypeStruct(sh, d) for sh, d in outs],
        in_specs=[far] * len(arrays) + [vmem],
        out_specs=[vmem] * len(outs),
        scratch_shapes=[pltpu.VMEM((count * width, S), F32)] * len(arrays)
        + [pltpu.SemaphoreType.DMA((len(arrays),))],
        compiler_params=pltpu.CompilerParams(vmem_limit_bytes=16 << 20),
        cost_estimate=pl.CostEstimate(flops=1000, bytes_accessed=3_000_000, transcendentals=0),
    )(*arrays, orders)


def prep(level, leads, coups, orders):
    lead = 3 if level == 3 else 2
    tgh, tgl, hot = prep_part(level, leads, 0, lead, orders, True)
    kh, kl = prep_part(level, coups, lead, 7 - lead, orders, False)
    return tgh, tgl, kh, kl, hot


def first_kernel(v_ref, ord_ref, t_ref, g_ref, s_ref, y_ref):
    a = select(v_ref[...], one_hot(ord_ref, 0), NN)
    s0 = a[:, :S]
    w = a[:, S:] - mm(s0, *split(t_ref[...]), NN)
    s_ref[...] = s0
    y_ref[...] = mm(w, *split(g_ref[...]), NN)


def reduce_kernel(level, own_ref, got_ref, hot, tgh, tgl, s_ref, y_ref):
    b = bits()[level - 1]
    own, got = own_ref[...], got_ref[...]
    lower = jnp.where(b == 0, own, got)
    upper = jnp.where(b == 0, got, own)
    a = select(lower, hot[:S, :], NN) + select(upper, hot[S:, :], NN)
    s0 = a[:, :S]
    w = a[:, S:] - mm(s0, tgh[0], tgl[0], NT)
    s_ref[...] = s0
    y_ref[...] = mm(w, tgh[1], tgl[1], NT)


def own_kernel(dims, s_ref, y_ref, kh, kl, o_ref):
    o_ref[...] = s_ref[...] - mm(y_ref[...], kh[0], kl[0], dims)


def couple(level, acc, got, kh, kl, dims):
    for ref, k in zip(got, sides(level)):
        acc = acc - mm(ref[...], kh[k], kl[k], dims)
    return acc


def couple0_kernel(acc_ref, g0, g1, g2, g3, kh, kl, keep_ref, send_ref, full):
    full[...] = couple(0, acc_ref[...], (g0, g1, g2, g3), kh, kl, NN)
    b = bits()[0]
    keep_ref[...] = full[pl.ds(pl.multiple_of(b * 64, 64), 64), :]
    send_ref[...] = full[pl.ds(pl.multiple_of((1 - b) * 64, 64), 64), :]


def couple_kernel(level, acc_ref, g0, g1, g2, g3, kh, kl, o_ref):
    o_ref[...] = couple(level, acc_ref[...], (g0, g1, g2, g3), kh, kl, NT)


def root_kernel(acc_ref, g0, g1, g2, kh, kl, tgh, tgl, t_ref, *q_refs):
    skeleton = couple(3, acc_ref[...], (g0, g1, g2), kh, kl, NT)
    t = mm(skeleton, tgh[2], tgl[2], NT)
    t_ref[...] = t
    spread(3, t, kh, kl, q_refs, NN)


def spread(level, t, kh, kl, q_refs, dims):
    for ref, k in zip(q_refs, sides(level)):
        ref[...] = mm(t, kh[k], kl[k], dims)


def own_back_kernel(dims, t_ref, kh, kl, o_ref):
    o_ref[...] = mm(t_ref[...], kh[0], kl[0], dims)


def solve(t, y, q0, got, tgh, tgl, dims):
    u = q0
    for ref in got:
        u = u + ref[...]
    xr = y - mm(u, tgh[1], tgl[1], dims)
    xs = t - mm(xr, tgh[0], tgl[0], dims)
    return jnp.concatenate([xs, xr], 1)


def down_kernel(level, n_got, *refs):
    t_ref, y_ref, q0_ref = refs[:3]
    got = refs[3 : 3 + n_got]
    tgh, tgl, hot, kh, kl, o_ref, *q_refs = refs[3 + n_got :]
    both = solve(t_ref[...], y_ref[...], q0_ref[...], got, tgh, tgl, NN)
    b = bits()[level - 1]
    half = hot[pl.ds(pl.multiple_of(b * S, S), S), :]
    t = select(both, half, NT)
    o_ref[...] = t
    spread(level - 1, t, kh, kl, q_refs, NN)


def down1_kernel(t_ref, y_ref, q0_ref, g0, g1, g2, g3, tgh, tgl, hot, keep_ref, send_ref):
    both = solve(t_ref[...], y_ref[...], q0_ref[...], (g0, g1, g2, g3), tgh, tgl, NN)
    b = bits()[0]
    send_ref[...] = select(both, hot[pl.ds(pl.multiple_of((1 - b) * S, S), S), :], NT)
    keep_ref[...] = select(both, hot[pl.ds(pl.multiple_of(b * S, S), S), :], NT)


def spread0_kernel(keep_ref, got_ref, kh, kl, t_ref, *q_refs):
    b = bits()[0]
    keep, got = keep_ref[...], got_ref[...]
    t = jnp.concatenate([jnp.where(b == 0, keep, got), jnp.where(b == 0, got, keep)], 0)
    t_ref[...] = t
    spread(0, t, kh, kl, q_refs, NT)


def last_kernel(t_ref, y_ref, q0_ref, g0, g1, g2, g3, tgh, tgl, hot, o_ref):
    both = solve(t_ref[...], y_ref[...], q0_ref[...], (g0, g1, g2, g3), tgh, tgl, NT)
    o_ref[...] = select(both, hot[...], NT)


def paired(x, axis, distance, odd):
    n = lax.axis_size(axis)
    shift = distance if odd else 0
    route = [(i, ((i + shift) ^ distance) - shift) for i in range(n)]
    return lax.ppermute(x, axis, [(i, k) for i, k in route if 0 <= k < n])


def halo(level, fields):
    dx, dy = 1 << SHIFT_X[level], 1 << SHIFT_Y[level]
    if level == 3:
        return [
            paired(fields[0], "bx", dx, False),
            paired(fields[1], "bx", dx, True),
            paired(fields[2], "by", dy, False),
        ]
    return [
        paired(fields[0], "bx", dx, False),
        paired(fields[1], "bx", dx, True),
        paired(fields[2], "by", dy, False),
        paired(fields[3], "by", dy, True),
    ]


def core_swap(x):
    return paired(x, "by", 1, False)


def x_swap(x):
    return paired(x, "bx", 1, False)


def z_swap(x):
    return paired(x, "by", 2, False)


def gather_pairs(x, axis, distance):
    n = lax.axis_size(axis)
    groups = [[i, i ^ distance] for i in range(n) if i < i ^ distance]
    return lax.all_gather(x, axis, axis_index_groups=groups)


def after(x, event):
    return lax.optimization_barrier((x, event))[0]


def masked(mask):
    return lambda piece: piece ^ mask


def body(rhs, order, i0, i1, i2, i3, n0, n1, n2, n3, c0, c1, c2, c3, root):
    orders = order[0, 0]
    turned = lambda x: jnp.swapaxes(x[0, 0], -1, -2)
    w3 = pack3(*[turned(x) for x in (i3, n3, root, c3)])
    x3, z3 = x_swap(w3), z_swap(w3)

    m, h = (128, S), (64, S)
    s0, y0 = call(
        first_kernel, [(m, F32)] * 2, after(rhs[0, 0], w3), orders, i0[0, 0], n0[0, 0],
        fetch=(0, 1, 2, 3), room=59,
    )
    w12, lead2, coup2 = pack12(*[turned(x) for x in (after(i1, y0), n1, c1, i2, n2, c2)])
    tgh0, tgl0, kh0, kl0, hot0 = call(
        prep0_kernel,
        [((2, S, S), BF16)] * 2 + [((5, S, S), BF16)] * 2 + [((2 * S, 2 * S), BF16)],
        i0[0, 0], n0[0, 0], c0[0, 0], after(orders, y0),
        fetch=(0, 1, 2, 3),
    )
    y0, x3, z3, w12, kh0 = lax.optimization_barrier((y0, x3, z3, w12, kh0))
    c12 = core_swap(w12)
    got = halo(0, [y0] * 4)
    (acc,) = call(functools.partial(own_kernel, NN), [(m, F32)], s0, y0, kh0, kl0)
    keep, send = call(couple0_kernel, [(h, F32)] * 2, acc, *got, kh0, kl0, scratch=[(m, F32)])
    lead2x, zx3 = x_swap(after(lead2, got)), z_swap(after(x3, got))
    pieces = [(0, w12, 0), (1, c12, 0)]
    ready = {1: prep(1, pieces, pieces, orders)}

    kept = {0: y0}
    own, other = keep, core_swap(send)
    for level in (1, 2, 3):
        tgh, tgl, kh, kl, hot = ready[level]
        s, y = call(
            functools.partial(reduce_kernel, level), [(h, F32)] * 2, own, other, hot, tgh, tgl
        )
        if level == 1:
            y, lead2x = lax.optimization_barrier((y, lead2x))
        kept[level] = y
        if level == 2:
            coup2x = x_swap(after(coup2, other))
        got = halo(level, [y] * 4)
        if level == 2:
            first = -2 * (S >> 2)
            coups = near + [(2, coup2x, first), (3, core_swap(after(coup2x, got)), first)]
            kh, kl = prep_part(2, coups, 2, 5, orders, False)
            ready[2] = (tgh, tgl, kh, kl, hot)
        (acc,) = call(functools.partial(own_kernel, NT), [(h, F32)], s, y, kh, kl)
        if level == 1:
            near = [(0, w12, ROWS[1]), (1, c12, ROWS[1])]
            lead2xc = core_swap(after(lead2x, acc))
            leads = near + [(2, lead2x, 0), (3, lead2xc, 0)]
            *lead_parts, hot2 = prep_part(2, leads, 0, 2, orders, True)
            ready[2] = (*lead_parts, None, None, hot2)
        if level == 2:
            pieces = [(2 * n, v, 0) for n, v in enumerate((w3, x3, z3, zx3))]
            pieces += [(m + 1, core_swap(after(v, got)), 0) for m, v, _ in pieces]
            ready[3] = prep(3, pieces, pieces, orders)
        if level < 3:
            (own,) = call(functools.partial(couple_kernel, level), [(h, F32)], acc, *got, kh, kl)
            if level == 1:
                own, zx3, lead2xc = lax.optimization_barrier((own, zx3, lead2xc))
            other = x_swap(own) if level == 1 else z_swap(own)
    t, *q = call(root_kernel, [(h, F32)] * 4, acc, *got, kh, kl, tgh, tgl)
    for level in (3, 2):
        tgh, tgl, kh, kl, hot = ready[level]
        got = halo(level, q)
        (q0,) = call(functools.partial(own_back_kernel, NN), [(h, F32)], t, kh, kl)
        t, *q = call(
            functools.partial(down_kernel, level, len(got)),
            [(h, F32)] * 5,
            t, kept[level], q0, *got, tgh, tgl, hot, ready[level - 1][2], ready[level - 1][3],
        )
    tgh, tgl, kh, kl, hot = ready[1]
    got = halo(1, q)
    (q0,) = call(functools.partial(own_back_kernel, NN), [(h, F32)], t, kh, kl)
    keep, send = call(down1_kernel, [(h, F32)] * 2, t, kept[1], q0, *got, tgh, tgl, hot)
    t, *q = call(spread0_kernel, [(m, F32)] * 5, keep, core_swap(send), kh0, kl0)
    got = halo(0, q)
    (q0,) = call(functools.partial(own_back_kernel, NT), [(m, F32)], t, kh0, kl0)
    (x,) = call(last_kernel, [((128, 2 * S), F32)], t, kept[0], q0, *got, tgh0, tgl0, hot0)
    return x[None, None]


def solution(mesh):
    four = P("bx", "by", None, None)
    five = P("bx", "by", None, None, None)
    in_specs = (four,) * 10 + (five,) * 4 + (four,)
    return jax.shard_map(body, mesh=mesh, in_specs=in_specs, out_specs=four, check_vma=False)
```

```python
import functools

import jax
import jax.numpy as jnp
from jax import lax
from jax.experimental import pallas as pl
from jax.experimental.pallas import tpu as pltpu
from jax.sharding import PartitionSpec as P

F32 = jnp.float32
BF16 = jnp.bfloat16
AXES = ("bx", "by")
S = 384
NN = (((1,), (0,)), ((), ()))
NT = (((1,), (1,)), ((), ()))
SHIFT_X = (0, 0, 1, 1)
SHIFT_Y = (0, 1, 1, 2)


def split(x):
    hi = x.astype(BF16)
    return hi, (x - hi.astype(F32)).astype(BF16)


def mm(a, bh, bl, dims):
    rows = a.shape[0]
    ah, al = split(a)
    both = lax.dot_general(jnp.concatenate([ah, al], 0), bh, dims, preferred_element_type=F32)
    low = lax.dot_general(ah, bl, dims, preferred_element_type=F32)
    return both[:rows] + (both[rows:] + low)


def select(a, hot, dims):
    rows = a.shape[0]
    ah, al = split(a)
    both = lax.dot_general(jnp.concatenate([ah, al], 0), hot, dims, preferred_element_type=F32)
    return both[:rows] + both[rows:]


def bits():
    i, j = lax.axis_index("bx"), lax.axis_index("by")
    return j & 1, i & 1, (j >> 1) & 1


def sides(level):
    px = (lax.axis_index("bx") >> SHIFT_X[level]) & 1
    py = (lax.axis_index("by") >> SHIFT_Y[level]) & 1
    if level == 3:
        return 2 - px, 1 + px, 3
    return 2 - px, 1 + px, 4 - py, 3 + py


def call(body, outs, *args, fetch=(), scratch=(), room=16, flops=50_000_000, size=3_000_000):
    vmem, far = pl.BlockSpec(memory_space=pltpu.VMEM), pl.BlockSpec(memory_space=pltpu.HBM)
    n_in, n_out, n_own = len(args), len(outs), len(scratch)

    def kernel(*refs):
        ins = list(refs[:n_in])
        rest = refs[n_in : n_in + n_out + n_own]
        staged = refs[n_in + n_out + n_own :]
        if fetch:
            sems = staged[-1]
            copies = []
            for n, (at, buf) in enumerate(zip(fetch, staged)):
                copies.append(pltpu.make_async_copy(ins[at], buf, sems.at[n]))
                copies[-1].start()
                ins[at] = buf
            for copy in copies:
                copy.wait()
        body(*ins, *rest)

    own = [pltpu.VMEM(sh, d) for sh, d in scratch]
    own += [pltpu.VMEM(args[at].shape, args[at].dtype) for at in fetch]
    if fetch:
        own.append(pltpu.SemaphoreType.DMA((len(fetch),)))
    return pl.pallas_call(
        kernel,
        out_shape=[jax.ShapeDtypeStruct(s, d) for s, d in outs],
        in_specs=[far if n in fetch else vmem for n in range(n_in)],
        out_specs=[vmem] * n_out,
        scratch_shapes=own,
        compiler_params=pltpu.CompilerParams(vmem_limit_bytes=room << 20),
        cost_estimate=pl.CostEstimate(flops=flops, bytes_accessed=size, transcendentals=0),
    )(*args)


def one_hot(order_ref, level):
    order = order_ref[level : level + 1, :]
    return (lax.broadcasted_iota(jnp.int32, (2 * S, 2 * S), 0) == order).astype(F32).astype(BF16)


def prep0_kernel(t_ref, g_ref, k_ref, ord_ref, tgh, tgl, kh, kl, hot):
    for n, ref in enumerate((t_ref, g_ref)):
        tgh[n], tgl[n] = split(ref[...])
    for n in range(5):
        kh[n], kl[n] = split(k_ref[n])
    hot[...] = one_hot(ord_ref, 0)


ROWS = tuple(7 * (S >> level) for level in range(4))


def lay(out, row, blocks):
    for block in blocks:
        out[row : row + block.shape[0], :] = block
        row += block.shape[0]


def pack3_kernel(i3, n3, r3, c3, w3):
    far = 4 - ((lax.axis_index("by") >> SHIFT_Y[3]) & 1)
    lay(w3, 0, [i3[...], n3[...], r3[...]] + [c3[k] for k in range(3)] + [c3[far]])


def pack12_kernel(i1, n1, c1, i2, n2, c2, w12, lead2, coup2):
    lay(w12, 0, [i1[...], n1[...]] + [c1[k] for k in range(5)])
    lead, coup = [i2[...], n2[...]], [c2[k] for k in range(5)]
    lay(w12, ROWS[1], lead + coup)
    lay(lead2, 0, lead)
    lay(coup2, 0, coup)


def pack3(*arrays):
    return call(pack3_kernel, [((ROWS[3], S), F32)], *arrays, fetch=(0, 1, 2, 3), room=60, flops=1000)[0]


def pack12(*arrays):
    outs = [((rows, S), F32) for rows in (ROWS[1] + ROWS[2], 2 * (S >> 2), 5 * (S >> 2))]
    return call(pack12_kernel, outs, *arrays, fetch=tuple(range(6)), room=56, flops=1000)


def prep_kernel(level, places, base, count, hot_too, *refs):
    n_in = len(places)
    ins, ord_ref, (high, low, *hot) = refs[:n_in], refs[n_in], refs[n_in + 1 : n_in + 3 + hot_too]
    bufs, sems = refs[n_in + 3 + hot_too : -1], refs[-1]
    width = S >> level
    copies = [
        pltpu.make_async_copy(ref.at[pl.ds(row, count * width)], buf, sems.at[n])
        for n, (ref, buf, row) in enumerate(zip(ins, bufs, base))
    ]
    for copy in copies:
        copy.start()
    if hot_too:
        hot[0][...] = one_hot(ord_ref, level)
    b = bits()
    piece = b[0] + 2 * b[1] * (level > 1) + 4 * b[2] * (level > 2)
    for n, mask in enumerate(places):
        copies[n].wait()
        where = pl.ds(pl.multiple_of((piece ^ mask) * width, width), width)
        for m in range(count):
            hi, lo = split(bufs[n][m * width : (m + 1) * width, :])
            high[m, where, :], low[m, where, :] = hi, lo


def prep_part(level, pieces, first, count, orders, hot_too):
    width = S >> level
    arrays = [x for _, x, _ in pieces]
    base = [row + first * width for _, _, row in pieces]
    outs = [((count, S, S), BF16)] * 2 + [((2 * S, 2 * S), BF16)] * hot_too
    vmem, far = pl.BlockSpec(memory_space=pltpu.VMEM), pl.BlockSpec(memory_space=pltpu.HBM)
    places = [mask for mask, _, _ in pieces]
    return pl.pallas_call(
        functools.partial(prep_kernel, level, places, base, count, hot_too),
        out_shape=[jax.ShapeDtypeStruct(sh, d) for sh, d in outs],
        in_specs=[far] * len(arrays) + [vmem],
        out_specs=[vmem] * len(outs),
        scratch_shapes=[pltpu.VMEM((count * width, S), F32)] * len(arrays)
        + [pltpu.SemaphoreType.DMA((len(arrays),))],
        compiler_params=pltpu.CompilerParams(vmem_limit_bytes=16 << 20),
        cost_estimate=pl.CostEstimate(flops=1000, bytes_accessed=3_000_000, transcendentals=0),
    )(*arrays, orders)


def prep(level, leads, coups, orders):
    lead = 3 if level == 3 else 2
    tgh, tgl, hot = prep_part(level, leads, 0, lead, orders, True)
    kh, kl = prep_part(level, coups, lead, 7 - lead, orders, False)
    return tgh, tgl, kh, kl, hot


def first_kernel(v_ref, ord_ref, t_ref, g_ref, s_ref, y_ref):
    a = select(v_ref[...], one_hot(ord_ref, 0), NN)
    s0 = a[:, :S]
    w = a[:, S:] - mm(s0, *split(t_ref[...]), NN)
    s_ref[...] = s0
    y_ref[...] = mm(w, *split(g_ref[...]), NN)


def reduce_kernel(level, own_ref, got_ref, hot, tgh, tgl, s_ref, y_ref):
    b = bits()[level - 1]
    own, got = own_ref[...], got_ref[...]
    lower = jnp.where(b == 0, own, got)
    upper = jnp.where(b == 0, got, own)
    a = select(lower, hot[:S, :], NN) + select(upper, hot[S:, :], NN)
    s0 = a[:, :S]
    w = a[:, S:] - mm(s0, tgh[0], tgl[0], NT)
    s_ref[...] = s0
    y_ref[...] = mm(w, tgh[1], tgl[1], NT)


def own_kernel(dims, s_ref, y_ref, kh, kl, o_ref):
    o_ref[...] = s_ref[...] - mm(y_ref[...], kh[0], kl[0], dims)


def couple(level, acc, got, kh, kl, dims):
    for ref, k in zip(got, sides(level)):
        acc = acc - mm(ref[...], kh[k], kl[k], dims)
    return acc


def couple0_kernel(acc_ref, g0, g1, g2, g3, kh, kl, keep_ref, send_ref, full):
    full[...] = couple(0, acc_ref[...], (g0, g1, g2, g3), kh, kl, NN)
    b = bits()[0]
    keep_ref[...] = full[pl.ds(pl.multiple_of(b * 64, 64), 64), :]
    send_ref[...] = full[pl.ds(pl.multiple_of((1 - b) * 64, 64), 64), :]


def couple_kernel(level, acc_ref, g0, g1, g2, g3, kh, kl, o_ref):
    o_ref[...] = couple(level, acc_ref[...], (g0, g1, g2, g3), kh, kl, NT)


def root_kernel(acc_ref, g0, g1, g2, kh, kl, tgh, tgl, t_ref, *q_refs):
    skeleton = couple(3, acc_ref[...], (g0, g1, g2), kh, kl, NT)
    t = mm(skeleton, tgh[2], tgl[2], NT)
    t_ref[...] = t
    spread(3, t, kh, kl, q_refs, NN)


def spread(level, t, kh, kl, q_refs, dims):
    for ref, k in zip(q_refs, sides(level)):
        ref[...] = mm(t, kh[k], kl[k], dims)


def own_back_kernel(dims, t_ref, kh, kl, o_ref):
    o_ref[...] = mm(t_ref[...], kh[0], kl[0], dims)


def solve(t, y, q0, got, tgh, tgl, dims):
    u = q0
    for ref in got:
        u = u + ref[...]
    xr = y - mm(u, tgh[1], tgl[1], dims)
    xs = t - mm(xr, tgh[0], tgl[0], dims)
    return jnp.concatenate([xs, xr], 1)


def down_kernel(level, n_got, *refs):
    t_ref, y_ref, q0_ref = refs[:3]
    got = refs[3 : 3 + n_got]
    tgh, tgl, hot, kh, kl, o_ref, *q_refs = refs[3 + n_got :]
    both = solve(t_ref[...], y_ref[...], q0_ref[...], got, tgh, tgl, NN)
    b = bits()[level - 1]
    half = hot[pl.ds(pl.multiple_of(b * S, S), S), :]
    t = select(both, half, NT)
    o_ref[...] = t
    spread(level - 1, t, kh, kl, q_refs, NN)


def down1_kernel(t_ref, y_ref, q0_ref, g0, g1, g2, g3, tgh, tgl, hot, keep_ref, send_ref):
    both = solve(t_ref[...], y_ref[...], q0_ref[...], (g0, g1, g2, g3), tgh, tgl, NN)
    b = bits()[0]
    send_ref[...] = select(both, hot[pl.ds(pl.multiple_of((1 - b) * S, S), S), :], NT)
    keep_ref[...] = select(both, hot[pl.ds(pl.multiple_of(b * S, S), S), :], NT)


def spread0_kernel(keep_ref, got_ref, kh, kl, t_ref, *q_refs):
    b = bits()[0]
    keep, got = keep_ref[...], got_ref[...]
    t = jnp.concatenate([jnp.where(b == 0, keep, got), jnp.where(b == 0, got, keep)], 0)
    t_ref[...] = t
    spread(0, t, kh, kl, q_refs, NT)


def last_kernel(t_ref, y_ref, q0_ref, g0, g1, g2, g3, tgh, tgl, hot, o_ref):
    both = solve(t_ref[...], y_ref[...], q0_ref[...], (g0, g1, g2, g3), tgh, tgl, NT)
    o_ref[...] = select(both, hot[...], NT)


def paired(x, axis, distance, odd):
    n = lax.axis_size(axis)
    shift = distance if odd else 0
    route = [(i, ((i + shift) ^ distance) - shift) for i in range(n)]
    return lax.ppermute(x, axis, [(i, k) for i, k in route if 0 <= k < n])


def halo(level, fields):
    dx, dy = 1 << SHIFT_X[level], 1 << SHIFT_Y[level]
    along_y = [paired(f, "by", dy, odd) for f, odd in zip(fields[2:], (False, True)[: 2 - level // 3])]
    return [paired(f, "bx", dx, odd) for f, odd in zip(fields[:2], (False, True))] + along_y


def core_swap(x):
    return paired(x, "by", 1, False)


def x_swap(x):
    return paired(x, "bx", 1, False)


def z_swap(x):
    return paired(x, "by", 2, False)


def gather_pairs(x, axis, distance):
    n = lax.axis_size(axis)
    groups = [[i, i ^ distance] for i in range(n) if i < i ^ distance]
    return lax.all_gather(x, axis, axis_index_groups=groups)


def after(x, event):
    return lax.optimization_barrier((x, event))[0]


def masked(mask):
    return lambda piece: piece ^ mask


def body(rhs, order, i0, i1, i2, i3, n0, n1, n2, n3, c0, c1, c2, c3, root):
    orders = order[0, 0]
    turned = lambda x: jnp.swapaxes(x[0, 0], -1, -2)
    w3 = pack3(*[turned(x) for x in (i3, n3, root, c3)])
    x3, z3 = x_swap(w3), z_swap(w3)

    m, h = (128, S), (64, S)
    s0, y0 = call(
        first_kernel, [(m, F32)] * 2, after(rhs[0, 0], w3), orders, i0[0, 0], n0[0, 0],
        fetch=(0, 1, 2, 3), room=59,
    )
    w12, lead2, coup2 = pack12(*[turned(x) for x in (after(i1, y0), n1, c1, i2, n2, c2)])
    tgh0, tgl0, kh0, kl0, hot0 = call(
        prep0_kernel,
        [((2, S, S), BF16)] * 2 + [((5, S, S), BF16)] * 2 + [((2 * S, 2 * S), BF16)],
        i0[0, 0], n0[0, 0], c0[0, 0], after(orders, y0),
        fetch=(0, 1, 2, 3),
    )
    y0, x3, z3, w12, kh0 = lax.optimization_barrier((y0, x3, z3, w12, kh0))
    c12 = core_swap(w12)
    got = halo(0, [y0] * 4)
    (acc,) = call(functools.partial(own_kernel, NN), [(m, F32)], s0, y0, kh0, kl0)
    keep, send = call(couple0_kernel, [(h, F32)] * 2, acc, *got, kh0, kl0, scratch=[(m, F32)])
    lead2x, zx3 = x_swap(after(lead2, got)), z_swap(after(x3, got))
    pieces = [(0, w12, 0), (1, c12, 0)]
    ready = {1: prep(1, pieces, pieces, orders)}

    kept = {0: y0}
    own, other = keep, core_swap(send)
    for level in (1, 2, 3):
        tgh, tgl, kh, kl, hot = ready[level]
        s, y = call(
            functools.partial(reduce_kernel, level), [(h, F32)] * 2, own, other, hot, tgh, tgl
        )
        if level == 1:
            y, lead2x = lax.optimization_barrier((y, lead2x))
        kept[level] = y
        if level == 2:
            coup2x = x_swap(after(coup2, other))
        got = halo(level, [y] * 4)
        if level == 2:
            first = -2 * (S >> 2)
            coups = near + [(2, coup2x, first), (3, core_swap(after(coup2x, got)), first)]
            kh, kl = prep_part(2, coups, 2, 5, orders, False)
            ready[2] = (tgh, tgl, kh, kl, hot)
        (acc,) = call(functools.partial(own_kernel, NT), [(h, F32)], s, y, kh, kl)
        if level == 1:
            near = [(0, w12, ROWS[1]), (1, c12, ROWS[1])]
            lead2xc = core_swap(after(lead2x, acc))
            leads = near + [(2, lead2x, 0), (3, lead2xc, 0)]
            *lead_parts, hot2 = prep_part(2, leads, 0, 2, orders, True)
            ready[2] = (*lead_parts, None, None, hot2)
        if level == 2:
            pieces = [(2 * n, v, 0) for n, v in enumerate((w3, x3, z3, zx3))]
            pieces += [(m + 1, core_swap(after(v, got)), 0) for m, v, _ in pieces]
            ready[3] = prep(3, pieces, pieces, orders)
        if level < 3:
            (own,) = call(functools.partial(couple_kernel, level), [(h, F32)], acc, *got, kh, kl)
            if level == 1:
                own, zx3, lead2xc = lax.optimization_barrier((own, zx3, lead2xc))
            other = x_swap(own) if level == 1 else z_swap(own)
    t, *q = call(root_kernel, [(h, F32)] * 4, acc, *got, kh, kl, tgh, tgl)
    for level in (3, 2):
        tgh, tgl, kh, kl, hot = ready[level]
        got = halo(level, q)
        (q0,) = call(functools.partial(own_back_kernel, NN), [(h, F32)], t, kh, kl)
        t, *q = call(
            functools.partial(down_kernel, level, len(got)),
            [(h, F32)] * 5,
            t, kept[level], q0, *got, tgh, tgl, hot, ready[level - 1][2], ready[level - 1][3],
        )
    tgh, tgl, kh, kl, hot = ready[1]
    got = halo(1, q)
    (q0,) = call(functools.partial(own_back_kernel, NN), [(h, F32)], t, kh, kl)
    keep, send = call(down1_kernel, [(h, F32)] * 2, t, kept[1], q0, *got, tgh, tgl, hot)
    t, *q = call(spread0_kernel, [(m, F32)] * 5, keep, core_swap(send), kh0, kl0)
    got = halo(0, q)
    (q0,) = call(functools.partial(own_back_kernel, NT), [(m, F32)], t, kh0, kl0)
    (x,) = call(last_kernel, [((128, 2 * S), F32)], t, kept[0], q0, *got, tgh0, tgl0, hot0)
    return x[None, None]


def solution(mesh):
    four = P("bx", "by", None, None)
    five = P("bx", "by", None, None, None)
    in_specs = (four,) * 10 + (five,) * 4 + (four,)
    return jax.shard_map(body, mesh=mesh, in_specs=in_specs, out_specs=four, check_vma=False)
```
